256 devices in a mesh: lane: 64 (over y_hi, x, z), group: 4 (over y_lo, core).
Axes of the slice: x: 4, y: 4 (y_hi: 2, y_lo: 2; y = y_hi * 2 + y_lo), z: 8, core: 2. Of those that a mesh axis runs over, the one named last changes fastest.
Arguments:
- half_vectors: bfloat16 [2048, 768, 512], P('lane', None, 'group'), may hold values from -2.5 to 2.5
- mo_coeff: bfloat16 [768, 512], replicated, may hold values from -0.21875 to 0.21875
- amplitudes: bfloat16 [512, 4, 128, 512], P('group', None, 'lane'), may hold values from -0.01171875 to 0.01171875
Outputs:
- ladder: float32 [512, 4, 512], P('lane', None, 'group')
The draws below stay inside these ranges and needn't reach their ends.
All inputs are finite; a program needn't handle non-finite values.
Results may differ from the reference program's by a relative error of at most 0.0049.
Values may be sent and summed in bfloat16 or wider, within the bound.
No kernel may reach another device: no remote copies, remote signals or barrier semaphores. Data moves between devices by JAX's collectives and lax.ppermute only.
A program may use at most 128 MiB of HBM per device.

```python
import jax
import jax.numpy as jnp
from jax import lax

V = 512
NAO = 768
NL = 2048
AROWS = 4
P_SIZE = 512
NG = 4
DL = 128


def block_levels(rng, dims, shards, low, high):
    def one(dim, blocks):
        steps = jax.random.uniform(jax.random.fold_in(jax.random.fold_in(rng, 6), dim), (blocks,), jnp.float32, low / len(shards), high / len(shards))
        return jnp.repeat(jnp.exp(steps), dims[dim] // blocks).reshape((-1,) + (1,) * (len(dims) - dim - 1))

    loudness = one(*shards[0])
    for cut in shards[1:]:
        loudness = loudness * one(*cut)
    return loudness


def centred(rng, shape, scale, bound, split=(), kind=jnp.bfloat16):
    gain = block_levels(rng, shape, split, -0.22, 0.18) if split else 1.0
    values = jax.random.normal(rng, shape, jnp.float32) * scale * gain
    return jnp.minimum(jnp.maximum(values, -bound), bound).astype(kind)


def setup_inputs(seed: int = 0) -> dict:
    arg_keys = jax.random.split(jax.random.key(seed), 4)
    half_vectors = centred(arg_keys[0], (NL, NAO, V), 0.18, 2.5, ((0, 64), (2, 4)))
    mo_coeff = centred(arg_keys[1], (NAO, V), NAO ** -0.5, 0.21875)
    amplitudes = centred(arg_keys[2], (V, NG, DL, P_SIZE), (V * V) ** -0.5, 0.01171875, ((0, 4), (2, 64)))
    return dict(half_vectors=half_vectors, mo_coeff=mo_coeff, amplitudes=amplitudes)


def reference(half_vectors, mo_coeff, amplitudes):
    width = 32
    count = V // width
    coeff_full = mo_coeff.astype(jnp.float32)
    amp_full = amplitudes.reshape(V, V, P_SIZE)

    def pair_block(index):
        half_part = lax.dynamic_slice_in_dim(half_vectors, index * width, width, 2).astype(jnp.float32)
        rows = jnp.einsum("lmc,ma->lac", half_part, coeff_full[:, :AROWS])
        return rows.astype(jnp.bfloat16)

    pair_parts = lax.map(pair_block, jnp.arange(count, dtype=jnp.int32))
    pair_rows = jnp.transpose(pair_parts, (1, 2, 0, 3)).reshape(NL, AROWS, V)
    pair_rows = lax.optimization_barrier(pair_rows).astype(jnp.float32)

    def column_step(running, index):
        half_part = lax.dynamic_slice_in_dim(half_vectors, index * width, width, 2).astype(jnp.float32)
        columns = jnp.einsum("lmd,mb->dlb", half_part, coeff_full).astype(jnp.bfloat16)
        columns = lax.optimization_barrier(columns).astype(jnp.float32)
        integral = jnp.einsum("lac,dlb->cdab", pair_rows, columns).astype(jnp.bfloat16)
        integral = lax.optimization_barrier(integral).astype(jnp.float32)
        amp_slice = lax.dynamic_slice_in_dim(amp_full, index * width, width, 1).astype(jnp.float32)
        return running + jnp.einsum("cdab,cdp->pab", integral, amp_slice), None

    start_sum = jnp.zeros((P_SIZE, AROWS, V), jnp.float32)
    ladder, unused = lax.scan(column_step, start_sum, jnp.arange(count, dtype=jnp.int32))
    return ladder
```

```python
import jax
import jax.numpy as jnp
from jax import lax
from jax.experimental import pallas as pl
from jax.experimental.pallas import tpu as pltpu
from jax.sharding import Mesh, PartitionSpec as P

AROWS = 4
LANE = ("yh", "x", "z")
GROUP = ("yl", "co")
EVERY = LANE + GROUP
SIZES = {"yh": 2, "x": 4, "z": 8, "yl": 2, "co": 2}


def swap(block, axis, flip):
    count = 4 if isinstance(axis, tuple) else SIZES[axis]
    return lax.ppermute(block, axis, [(i, i ^ flip) for i in range(count)])


def double(block, axis, flip):
    return jnp.concatenate([block, swap(block, axis, flip)], axis=0)


def vec_kernel(half_ref, mo_ref, send_ref, pair_ref, rows):
    step, _, nc = half_ref.shape
    lanes, groups, dl, _, nb = send_ref.shape
    for i in range(step):
        full = lax.dot_general(
            half_ref[i], mo_ref[...], (((0,), (0,)), ((), ())),
            preferred_element_type=jnp.float32,
        )
        for g in range(groups):
            rows[g, i * nc : (i + 1) * nc, :] = full[:, g * nb : (g + 1) * nb]
        first = jnp.transpose(full[:, :nb])
        pair_ref[:, i, :] = first[:AROWS].astype(pair_ref.dtype)

    @pl.loop(0, lanes)
    def _(lane):
        for j in range(dl):
            for g in range(groups):
                piece = rows[g, pl.ds(lane * dl + j, step, stride=nc), :]
                send_ref[lane, g, j] = piece.astype(send_ref.dtype)


def make_vec(half, mo, lanes, groups):
    nl, nao, nc = half.shape
    nv = mo.shape[1]
    dl, nb = nc // lanes, nv // groups
    step = nl // 2
    return pl.pallas_call(
        vec_kernel,
        grid=(2,),
        in_specs=[
            pl.BlockSpec((step, nao, nc), lambda i: (i, 0, 0)),
            pl.BlockSpec((nao, nv), lambda i: (0, 0)),
        ],
        out_specs=[
            pl.BlockSpec((lanes, groups, dl, step, nb), lambda i: (0, 0, 0, i, 0)),
            pl.BlockSpec((AROWS, step, nc), lambda i: (0, i, 0)),
        ],
        out_shape=[
            jax.ShapeDtypeStruct((lanes, groups, dl, nl, nb), jnp.bfloat16),
            jax.ShapeDtypeStruct((AROWS, nl, nc), jnp.float32),
        ],
        scratch_shapes=[pltpu.VMEM((groups, step * nc, nb), jnp.float32)],
        name="vec",
    )(half, mo)


def ladder_kernel(where_ref, got_ref, pair_ref, amp_ref, out_ref, turned, panels, total):
    half, arow = pl.program_id(0), pl.program_id(1)
    nyh, nx, nz, nyl, nco, dl, nl, nb = got_ref.shape
    nd = nyl * nco * dl
    nc = pair_ref.shape[-1]
    run = nz * nl
    at_yh, at_x, at_z = where_ref[0], where_ref[1], where_ref[2]

    @pl.when((half == 0) & (arow == 0))
    def _():
        total[...] = jnp.zeros_like(total)
        for sx in range(nx):
            for sy in range(nyh):
                column = (sx * nyh + sy) * run
                for d in range(nd):
                    yl, co, j = d // (nco * dl), d // dl % nco, d % dl
                    parts = [
                        got_ref[at_yh ^ sy, at_x ^ sx, at_z ^ sz, yl, co, j] for sz in range(nz)
                    ]
                    turned[d * nb : (d + 1) * nb, column : column + run] = jnp.transpose(
                        jnp.concatenate(parts, axis=0)
                    )

    weights = jnp.concatenate(
        [pair_ref[co, 0, :, :, :, 0].reshape(nx * nyh * run, nc) for co in range(nco)], axis=1
    )
    panel = jnp.dot(turned[...], weights, preferred_element_type=jnp.float32)
    panel = panel.astype(jnp.bfloat16)
    row = pl.multiple_of(arow * nb, nb)
    for co in range(nco):
        for d in range(nd):
            panels[pl.ds(row, nb), (co * nd + d) * nc : (co * nd + d + 1) * nc] = panel[
                d * nb : (d + 1) * nb, co * nc : (co + 1) * nc
            ]

    @pl.when(arow == AROWS - 1)
    def _():
        amps = amp_ref[:, 0].reshape(nco * nd * nc, amp_ref.shape[-1])
        total[...] += jnp.dot(panels[...], amps, preferred_element_type=jnp.float32)

    @pl.when((half == nyl - 1) & (arow == AROWS - 1))
    def _():
        out_ref[...] = jnp.transpose(total[...].astype(jnp.bfloat16))


def make_ladder(where, got, pair, amp):
    nyh, nx, nz, nyl, nco, dl, nl, nb = got.shape
    nc = pair.shape[-1]
    nd, npair = amp.shape[2], amp.shape[4]
    deep = nyh * nx * nz * nl
    return pl.pallas_call(
        ladder_kernel,
        grid_spec=pltpu.PrefetchScalarGridSpec(
            num_scalar_prefetch=1,
            grid=(nyl, AROWS),
            in_specs=[
                pl.BlockSpec(got.shape, lambda h, a, w: (0,) * 8, pipeline_mode=pl.Buffered(1)),
                pl.BlockSpec(
                    (nco, 1, nx, nyh, nz, 1, nl, nc), lambda h, a, w: (0, h, 0, 0, 0, a, 0, 0)
                ),
                pl.BlockSpec((nco, 1, nd, nc, npair), lambda h, a, w: (0, h, 0, 0, 0)),
            ],
            out_specs=pl.BlockSpec((npair, AROWS * nb), lambda h, a, w: (0, 0)),
            scratch_shapes=[
                pltpu.VMEM((nd * nb, deep), jnp.bfloat16),
                pltpu.VMEM((AROWS * nb, nco * nd * nc), jnp.bfloat16),
                pltpu.VMEM((AROWS * nb, npair), jnp.float32),
            ],
        ),
        out_shape=jax.ShapeDtypeStruct((npair, AROWS * nb), jnp.bfloat16),
        name="ladder",
    )(where, got, pair, amp)


def body(half, mo, amp):
    nl, nao, nc = half.shape
    nv = mo.shape[1]
    npair = amp.shape[3]
    lanes = SIZES["yh"] * SIZES["x"] * SIZES["z"]
    groups = SIZES["yl"] * SIZES["co"]
    dl, nb = nc // lanes, nv // groups

    send, pair = make_vec(half, mo, lanes, groups)
    pair = pair.astype(jnp.bfloat16)
    got = lax.all_to_all(
        send.reshape(lanes * groups, dl * nl, nb), EVERY, 0, 0, tiled=True
    ).reshape(2, 4, 8, 2, 2, dl, nl, nb)

    amp = jnp.transpose(amp.reshape(nc, groups * dl, npair), (1, 0, 2))[None]
    amp = double(amp, "yl", 1)[None]

    pair = pair[None]
    pair = double(pair, "z", 1)
    pair = double(pair, "z", 2)
    pair = double(pair, "z", 4)
    pair = pair[None]
    far = swap(pair, ("yh", "yl"), 2)
    near = swap(pair, ("yh", "yl"), 1)
    cross = swap(pair, ("yh", "yl"), 3)
    pair = jnp.concatenate([pair, far, near, cross], axis=0)
    pair = pair.reshape((1, 2, 2) + pair.shape[1:])
    pair, amp = lax.optimization_barrier((pair, amp))
    amp = double(amp, "co", 1)
    one = swap(pair, "x", 1)
    three = swap(pair, "x", 3)
    two_left = swap(three[:, :1], "x", 1)
    two_right = swap(one[:, 1:], "x", 3)
    two = jnp.concatenate([two_left, two_right], axis=1)
    pair = jnp.concatenate([pair, one, two, three], axis=0)
    pair = jnp.transpose(pair, (1, 0, 2, 3, 4, 5, 6))[None]
    pair = double(pair, "co", 1)

    where = jnp.stack([lax.axis_index("yh"), lax.axis_index("x"), lax.axis_index("z")])
    part = make_ladder(where.astype(jnp.int32), got, pair, amp)
    part = lax.all_to_all(
        part.reshape(lanes, npair // lanes, AROWS * nb), LANE, 0, 0, tiled=True
    )
    part = jnp.sum(part.astype(jnp.float32), axis=0)
    return part.reshape(npair // lanes, AROWS, nb)


def solution(mesh):
    fine = Mesh(mesh.devices.reshape(tuple(SIZES.values())), EVERY)
    in_specs = (P(LANE, None, GROUP), P(), P(GROUP, None, LANE, None))
    out_specs = P(LANE, None, GROUP)
    return jax.shard_map(
        body, mesh=fine, in_specs=in_specs, out_specs=out_specs, check_vma=False
    )
```

```python
import jax
import jax.numpy as jnp
from jax import lax
from jax.experimental import pallas as pl
from jax.experimental.pallas import tpu as pltpu
from jax.sharding import Mesh, PartitionSpec as P

AROWS = 4
LANE = ("yh", "x", "z")
GROUP = ("yl", "co")
EVERY = LANE + GROUP
UNROLL = 4
SIZES = {"yh": 2, "x": 4, "z": 8, "yl": 2, "co": 2}


def swap(block, axis, flip):
    count = 4 if isinstance(axis, tuple) else SIZES[axis]
    return lax.ppermute(block, axis, [(i, i ^ flip) for i in range(count)])


def double(block, axis, flip):
    return jnp.concatenate([block, swap(block, axis, flip)], axis=0)


def vec_kernel(half_ref, mo_ref, *refs):
    send_ref, rows = refs[-2:]
    step, _, nc = half_ref.shape
    lanes, groups, dl, _, nb = send_ref.shape
    for i in range(step):
        full = lax.dot_general(
            half_ref[i], mo_ref[...], (((0,), (0,)), ((), ())),
            preferred_element_type=jnp.float32,
        )
        for g in range(groups):
            rows[g, i * nc : (i + 1) * nc, :] = full[:, g * nb : (g + 1) * nb]

    @pl.loop(0, lanes, unroll=UNROLL)
    def _(lane):
        for j in range(dl):
            for g in range(groups):
                piece = rows[g, pl.ds(lane * dl + j, step, stride=nc), :]
                send_ref[lane, g, j] = piece.astype(send_ref.dtype)


def make_vec(half, mo, lanes, groups, which, send=None):
    nl, nao, nc = half.shape
    nv = mo.shape[1]
    dl, nb = nc // lanes, nv // groups
    step = nl // 2
    ins = [
        pl.BlockSpec((step, nao, nc), lambda i: (which, 0, 0)),
        pl.BlockSpec((nao, nv), lambda i: (0, 0)),
    ]
    args = (half, mo)
    if send is not None:
        ins.append(pl.BlockSpec(memory_space=pl.ANY))
        args += (send,)
    return pl.pallas_call(
        vec_kernel,
        grid=(1,),
        in_specs=ins,
        out_specs=pl.BlockSpec((lanes, groups, dl, step, nb), lambda i: (0, 0, 0, which, 0)),
        out_shape=jax.ShapeDtypeStruct((lanes, groups, dl, nl, nb), jnp.bfloat16),
        scratch_shapes=[pltpu.VMEM((groups, step * nc, nb), jnp.float32)],
        input_output_aliases={2: 0} if send is not None else {},
        cost_estimate=pl.CostEstimate(
            flops=2 * step * nao * nc * nv, transcendentals=0, bytes_accessed=2 * step * (nao * nc + nc * nv)
        ),
        name="vec",
    )(*args)


def ladder_kernel(where_ref, got_ref, pair_ref, amp_ref, out_ref, turned, panels, total):
    half, arow = pl.program_id(0), pl.program_id(1)
    nyh, nx, nz, nyl, nco, dl, nl, nb = got_ref.shape
    nd = nyl * nco * dl
    nc = pair_ref.shape[-1]
    run = nz * nl
    at_yh, at_x, at_z = where_ref[0], where_ref[1], where_ref[2]

    @pl.when((half == 0) & (arow == 0))
    def _():
        total[...] = jnp.zeros_like(total)
        for sx in range(nx):
            for sy in range(nyh):
                column = (sx * nyh + sy) * run
                for d in range(nd):
                    yl, co, j = d // (nco * dl), d // dl % nco, d % dl
                    parts = [
                        got_ref[at_yh ^ sy, at_x ^ sx, at_z ^ sz, yl, co, j] for sz in range(nz)
                    ]
                    turned[d * nb : (d + 1) * nb, column : column + run] = jnp.transpose(
                        jnp.concatenate(parts, axis=0)
                    )

    weights = jnp.concatenate(
        [pair_ref[co, 0, :, :, :, 0].reshape(nx * nyh * run, nc) for co in range(nco)], axis=1
    )
    panel = jnp.dot(turned[...], weights, preferred_element_type=jnp.float32)
    panel = panel.astype(jnp.bfloat16)
    row = pl.multiple_of(arow * nb, nb)
    for co in range(nco):
        for d in range(nd):
            panels[pl.ds(row, nb), (co * nd + d) * nc : (co * nd + d + 1) * nc] = panel[
                d * nb : (d + 1) * nb, co * nc : (co + 1) * nc
            ]

    @pl.when(arow == AROWS - 1)
    def _():
        amps = amp_ref[:, 0].reshape(nco * nd * nc, amp_ref.shape[-1])
        total[...] += jnp.dot(panels[...], amps, preferred_element_type=jnp.float32)

    @pl.when((half == nyl - 1) & (arow == AROWS - 1))
    def _():
        out_ref[...] = jnp.transpose(total[...].astype(jnp.bfloat16))


def make_ladder(where, got, pair, amp):
    nyh, nx, nz, nyl, nco, dl, nl, nb = got.shape
    nc = pair.shape[-1]
    nd, npair = amp.shape[2], amp.shape[4]
    deep = nyh * nx * nz * nl
    return pl.pallas_call(
        ladder_kernel,
        grid_spec=pltpu.PrefetchScalarGridSpec(
            num_scalar_prefetch=1,
            grid=(nyl, AROWS),
            in_specs=[
                pl.BlockSpec(got.shape, lambda h, a, w: (0,) * 8, pipeline_mode=pl.Buffered(1)),
                pl.BlockSpec(
                    (nco, 1, nx, nyh, nz, 1, nl, nc), lambda h, a, w: (0, h, 0, 0, 0, a, 0, 0)
                ),
                pl.BlockSpec((nco, 1, nd, nc, npair), lambda h, a, w: (0, h, 0, 0, 0)),
            ],
            out_specs=pl.BlockSpec((npair, AROWS * nb), lambda h, a, w: (0, 0)),
            scratch_shapes=[
                pltpu.VMEM((nd * nb, deep), jnp.bfloat16),
                pltpu.VMEM((AROWS * nb, nco * nd * nc), jnp.bfloat16),
                pltpu.VMEM((AROWS * nb, npair), jnp.float32),
            ],
        ),
        out_shape=jax.ShapeDtypeStruct((npair, AROWS * nb), jnp.bfloat16),
        name="ladder",
    )(where, got, pair, amp)


def body(half, mo, amp):
    nl, nao, nc = half.shape
    nv = mo.shape[1]
    npair = amp.shape[3]
    lanes = SIZES["yh"] * SIZES["x"] * SIZES["z"]
    groups = SIZES["yl"] * SIZES["co"]
    dl, nb = nc // lanes, nv // groups

    amp = jnp.transpose(amp.reshape(nc, groups * dl, npair), (1, 0, 2))[None]
    amp_far = swap(amp, "yl", 1)

    pair = jnp.einsum("lmc,ma->alc", half, mo[:, :AROWS], preferred_element_type=jnp.float32)
    pair = pair.astype(jnp.bfloat16)[None]
    half, pair, amp = lax.optimization_barrier((half, pair, amp))
    send = make_vec(half, mo, lanes, groups, 0)
    pair = double(pair, "z", 1)
    send, pair = lax.optimization_barrier((send, pair))
    send = make_vec(half, mo, lanes, groups, 1, send)
    pair = double(pair, "z", 2)
    pair = double(pair, "z", 4)
    send, pair, amp_far = lax.optimization_barrier((send, pair, amp_far))
    got = lax.all_to_all(
        send.reshape(lanes * groups, dl * nl, nb), EVERY, 0, 0, tiled=True
    ).reshape(2, 4, 8, 2, 2, dl, nl, nb)
    pair = pair[None]
    far = swap(pair, ("yh", "yl"), 2)
    near = swap(pair, ("yh", "yl"), 1)
    cross = swap(pair, ("yh", "yl"), 3)
    pair = jnp.concatenate([pair, far, near, cross], axis=0)
    pair = pair.reshape((1, 2, 2) + pair.shape[1:])
    amp = jnp.concatenate([amp, amp_far], axis=0)[None]
    pair, amp = lax.optimization_barrier((pair, amp))
    amp = double(amp, "co", 1)
    one = swap(pair, "x", 1)
    three = swap(pair, "x", 3)
    two_left = swap(three[:, :1], "x", 1)
    two_right = swap(one[:, 1:], "x", 3)
    two = jnp.concatenate([two_left, two_right], axis=1)
    pair = jnp.concatenate([pair, one, two, three], axis=0)
    pair = jnp.transpose(pair, (1, 0, 2, 3, 4, 5, 6))[None]
    pair = double(pair, "co", 1)

    where = jnp.stack([lax.axis_index("yh"), lax.axis_index("x"), lax.axis_index("z")])
    part = make_ladder(where.astype(jnp.int32), got, pair, amp)
    part = lax.all_to_all(
        part.reshape(lanes, npair // lanes, AROWS * nb), LANE, 0, 0, tiled=True
    )
    part = jnp.sum(part.astype(jnp.float32), axis=0)
    return part.reshape(npair // lanes, AROWS, nb)


def solution(mesh):
    fine = Mesh(mesh.devices.reshape(tuple(SIZES.values())), EVERY)
    in_specs = (P(LANE, None, GROUP), P(), P(GROUP, None, LANE, None))
    out_specs = P(LANE, None, GROUP)
    return jax.shard_map(
        body, mesh=fine, in_specs=in_specs, out_specs=out_specs, check_vma=False
    )
```

```python
import jax
import jax.numpy as jnp
from jax import lax
from jax.experimental import pallas as pl
from jax.experimental.pallas import tpu as pltpu
from jax.sharding import Mesh, PartitionSpec as P

AROWS = 4
LANE = ("yh", "x", "z")
GROUP = ("yl", "co")
EVERY = LANE + GROUP
UNROLL = 4
SIZES = {"yh": 2, "x": 4, "z": 8, "yl": 2, "co": 2}


def swap(block, axis, flip):
    count = 4 if isinstance(axis, tuple) else SIZES[axis]
    return lax.ppermute(block, axis, [(i, i ^ flip) for i in range(count)])


def double(block, axis, flip):
    return jnp.concatenate([block, swap(block, axis, flip)], axis=0)


def vec_kernel(half_ref, mo_ref, *refs):
    send_ref, rows = refs[-2:]
    step, _, nc = half_ref.shape
    lanes, groups, dl, _, nb = send_ref.shape
    for i in range(step):
        full = lax.dot_general(
            half_ref[i], mo_ref[...], (((0,), (0,)), ((), ())),
            preferred_element_type=jnp.float32,
        )
        for g in range(groups):
            rows[g, i * nc : (i + 1) * nc, :] = full[:, g * nb : (g + 1) * nb]

    @pl.loop(0, lanes, unroll=UNROLL)
    def _(lane):
        for j in range(dl):
            for g in range(groups):
                piece = rows[g, pl.ds(lane * dl + j, step, stride=nc), :]
                send_ref[lane, g, j] = piece.astype(send_ref.dtype)


def make_vec(half, mo, lanes, groups, which, send=None):
    nl, nao, nc = half.shape
    nv = mo.shape[1]
    dl, nb = nc // lanes, nv // groups
    step = nl // 2
    ins = [
        pl.BlockSpec((step, nao, nc), lambda i: (which, 0, 0)),
        pl.BlockSpec((nao, nv), lambda i: (0, 0)),
    ]
    args = (half, mo)
    if send is not None:
        ins.append(pl.BlockSpec(memory_space=pl.ANY))
        args += (send,)
    return pl.pallas_call(
        vec_kernel,
        grid=(1,),
        in_specs=ins,
        out_specs=pl.BlockSpec((lanes, groups, dl, step, nb), lambda i: (0, 0, 0, which, 0)),
        out_shape=jax.ShapeDtypeStruct((lanes, groups, dl, nl, nb), jnp.bfloat16),
        scratch_shapes=[pltpu.VMEM((groups, step * nc, nb), jnp.float32)],
        input_output_aliases={2: 0} if send is not None else {},
        cost_estimate=pl.CostEstimate(
            flops=2 * step * nao * nc * nv, transcendentals=0, bytes_accessed=2 * step * (nao * nc + nc * nv)
        ),
        name="vec",
    )(*args)


def ladder_kernel(where_ref, got_ref, *refs):
    pairs, amps = (refs[:5], refs[5:10]), refs[10:12]
    out_ref, turned, panels, total = refs[12:]
    half, arow = pl.program_id(0), pl.program_id(1)
    nyh, nx, nz, nyl, nco, dl, nl, nb = got_ref.shape
    nd = nyl * nco * dl
    nc, npair = amps[0].shape[-2:]
    run = nz * nl
    at_yh, at_x, at_z = where_ref[0], where_ref[1], where_ref[2]

    @pl.when((half == 0) & (arow == 0))
    def _():
        total[...] = jnp.zeros_like(total)
        for sx in range(nx):
            for sy in range(nyh):
                column = (sx * nyh + sy) * run
                for d in range(nd):
                    yl, co, j = d // (nco * dl), d // dl % nco, d % dl
                    parts = [
                        got_ref[at_yh ^ sy, at_x ^ sx, at_z ^ sz, yl, co, j] for sz in range(nz)
                    ]
                    turned[d * nb : (d + 1) * nb, column : column + run] = jnp.transpose(
                        jnp.concatenate(parts, axis=0)
                    )

    weights = jnp.concatenate(
        [
            jnp.concatenate([piece[0, :, :, 0].reshape(-1, nc) for piece in pieces], axis=0)
            for pieces in pairs
        ],
        axis=1,
    )
    panel = jnp.dot(turned[...], weights, preferred_element_type=jnp.float32)
    panel = panel.astype(jnp.bfloat16)
    row = pl.multiple_of(arow * nb, nb)
    for co in range(nco):
        for d in range(nd):
            panels[pl.ds(row, nb), (co * nd + d) * nc : (co * nd + d + 1) * nc] = panel[
                d * nb : (d + 1) * nb, co * nc : (co + 1) * nc
            ]

    @pl.when(arow == AROWS - 1)
    def _():
        for co in range(nco):
            total[...] += jnp.dot(
                panels[:, co * nd * nc : (co + 1) * nd * nc],
                amps[co][0].reshape(nd * nc, npair),
                preferred_element_type=jnp.float32,
            )

    @pl.when((half == nyl - 1) & (arow == AROWS - 1))
    def _():
        out_ref[...] = jnp.transpose(total[...].astype(jnp.bfloat16))


def make_ladder(where, got, pairs, amps):
    nyh, nx, nz, nyl, nco, dl, nl, nb = got.shape
    nd, nc, npair = amps[0].shape[1:]
    deep = nyh * nx * nz * nl
    return pl.pallas_call(
        ladder_kernel,
        grid_spec=pltpu.PrefetchScalarGridSpec(
            num_scalar_prefetch=1,
            grid=(nyl, AROWS),
            in_specs=[
                pl.BlockSpec(got.shape, lambda h, a, w: (0,) * 8, pipeline_mode=pl.Buffered(1)),
            ]
            + [
                pl.BlockSpec((1, p.shape[1], nz, 1, nl, nc), lambda h, a, w: (h, 0, 0, a, 0, 0))
                for p in pairs
            ]
            + [pl.BlockSpec((1, nd, nc, npair), lambda h, a, w: (h, 0, 0, 0))] * nco,
            out_specs=pl.BlockSpec((npair, AROWS * nb), lambda h, a, w: (0, 0)),
            scratch_shapes=[
                pltpu.VMEM((nd * nb, deep), jnp.bfloat16),
                pltpu.VMEM((AROWS * nb, nco * nd * nc), jnp.bfloat16),
                pltpu.VMEM((AROWS * nb, npair), jnp.float32),
            ],
        ),
        out_shape=jax.ShapeDtypeStruct((npair, AROWS * nb), jnp.bfloat16),
        name="ladder",
    )(where, got, *pairs, *amps)


def body(half, mo, amp):
    nl, nao, nc = half.shape
    nv = mo.shape[1]
    npair = amp.shape[3]
    lanes = SIZES["yh"] * SIZES["x"] * SIZES["z"]
    groups = SIZES["yl"] * SIZES["co"]
    dl, nb = nc // lanes, nv // groups

    amp = jnp.transpose(amp.reshape(nc, groups * dl, npair), (1, 0, 2))[None]
    amp_far = swap(amp, "yl", 1)

    pair = jnp.einsum("lmc,ma->alc", half, mo[:, :AROWS], preferred_element_type=jnp.float32)
    pair = pair.astype(jnp.bfloat16)[None]
    half, pair, amp = lax.optimization_barrier((half, pair, amp))
    send = make_vec(half, mo, lanes, groups, 0)
    pair = double(pair, "z", 1)
    send, pair = lax.optimization_barrier((send, pair))
    send = make_vec(half, mo, lanes, groups, 1, send)
    pair = double(pair, "z", 2)
    pair = double(pair, "z", 4)
    send, pair, amp_far = lax.optimization_barrier((send, pair, amp_far))
    got = lax.all_to_all(
        send.reshape(lanes * groups, dl * nl, nb), EVERY, 0, 0, tiled=True
    ).reshape(2, 4, 8, 2, 2, dl, nl, nb)
    pair = pair[None]
    far = swap(pair, ("yh", "yl"), 2)
    near = swap(pair, ("yh", "yl"), 1)
    cross = swap(pair, ("yh", "yl"), 3)
    pair = jnp.concatenate([pair, far, near, cross], axis=0)
    pair = pair.reshape((2, 2) + pair.shape[1:])
    amp = jnp.concatenate([amp, amp_far], axis=0)
    pair, amp = lax.optimization_barrier((pair, amp))
    amps = [amp, swap(amp, "co", 1)]
    one = swap(pair, "x", 1)
    three = swap(pair, "x", 3)
    two = [swap(three[:, :1], "x", 1), swap(one[:, 1:], "x", 3)]
    pieces = [pair, one, two[0], two[1], three]
    pairs = pieces + [swap(piece, "co", 1) for piece in pieces]

    where = jnp.stack([lax.axis_index("yh"), lax.axis_index("x"), lax.axis_index("z")])
    part = make_ladder(where.astype(jnp.int32), got, pairs, amps)
    part = lax.all_to_all(
        part.reshape(lanes, npair // lanes, AROWS * nb), LANE, 0, 0, tiled=True
    )
    part = jnp.sum(part.astype(jnp.float32), axis=0)
    return part.reshape(npair // lanes, AROWS, nb)


def solution(mesh):
    fine = Mesh(mesh.devices.reshape(tuple(SIZES.values())), EVERY)
    in_specs = (P(LANE, None, GROUP), P(), P(GROUP, None, LANE, None))
    out_specs = P(LANE, None, GROUP)
    return jax.shard_map(
        body, mesh=fine, in_specs=in_specs, out_specs=out_specs, check_vma=False
    )
```

```python
import jax
import jax.numpy as jnp
from jax import lax
from jax.experimental import pallas as pl
from jax.experimental.pallas import tpu as pltpu
from jax.sharding import Mesh, PartitionSpec as P


AROWS = 4
LANE = ("yh", "x", "z")
GROUP = ("yl", "co")
EVERY = LANE + GROUP
PHASES = 2
SIZES = {"yh": 2, "x": 4, "z": 8, "yl": 2, "co": 2}


def swap(block, axis, flip):
    count = 4 if isinstance(axis, tuple) else SIZES[axis]
    return lax.ppermute(block, axis, [(i, i ^ flip) for i in range(count)])


def double(block, axis, flip):
    return jnp.concatenate([block, swap(block, axis, flip)], axis=0)


def vec_kernel(half_ref, mo_ref, *refs):
    send_ref, rows = refs[-2:]
    part, _, nc = half_ref.shape
    lanes, groups, dl, step, nb = send_ref.shape
    now = pl.program_id(0)

    @pl.when(now < PHASES)
    def _():
        for i in range(part):
            full = lax.dot_general(
                half_ref[i], mo_ref[...], (((0,), (0,)), ((), ())),
                preferred_element_type=jnp.float32,
            )
            row = pl.multiple_of((now * part + i) * nc, nc)
            for g in range(groups):
                rows[g, pl.ds(row, nc), :] = full[:, g * nb : (g + 1) * nb]

    @pl.when(now >= PHASES)
    def _():
        first = (now - PHASES) * lanes * dl

        @pl.loop(0, lanes, unroll=8)
        def _(lane):
            for j in range(dl):
                for g in range(groups):
                    piece = rows[g, pl.ds(first + lane * dl + j, step, stride=nc), :]
                    send_ref[lane, g, j] = piece.astype(send_ref.dtype)


def make_vec(half, mo, lanes, groups, which, send=None):
    nl, nao, nc = half.shape
    nv = mo.shape[1]
    dl, nb = nc // lanes, nv // groups
    step = nl // 2
    ins = [
        pl.BlockSpec(
            (step // PHASES, nao, nc),
            lambda i: (which * PHASES + jnp.minimum(i, PHASES - 1), 0, 0),
        ),
        pl.BlockSpec((nao, nv), lambda i: (0, 0)),
    ]
    args = (half, mo)
    if send is not None:
        ins.append(pl.BlockSpec(memory_space=pl.ANY))
        args += (send,)
    return pl.pallas_call(
        vec_kernel,
        grid=(2 * PHASES,),
        in_specs=ins,
        out_specs=pl.BlockSpec(
            (lanes // PHASES, groups, dl, step, nb),
            lambda i: (jnp.maximum(i - PHASES, 0), 0, 0, which, 0),
        ),
        out_shape=jax.ShapeDtypeStruct((lanes, groups, dl, nl, nb), jnp.bfloat16),
        scratch_shapes=[pltpu.VMEM((groups, step * nc, nb), jnp.float32)],
        input_output_aliases={2: 0} if send is not None else {},
        cost_estimate=pl.CostEstimate(
            flops=2 * step * nao * nc * nv,
            transcendentals=0,
            bytes_accessed=2 * step * (nao * nc + nc * nv),
        ),
        name="vec",
    )(*args)


def ladder_kernel(where_ref, got_hbm, *refs):
    side_hbm, out_ref, got_ref, sides = refs[:12], refs[12], refs[13], refs[14:26]
    turned, panels, total, got_sem, side_sem = refs[26:]
    nyh, nx, nz, nyl, nco, dl, nl, nb = got_ref.shape
    nd = nyl * nco * dl
    nc, npair = sides[-1].shape[-2:]
    run = nz * nl
    at_yh, at_x, at_z = where_ref[0], where_ref[1], where_ref[2]

    def got_copy(sy, sx):
        at = (at_yh ^ sy, at_x ^ sx)
        return pltpu.make_async_copy(got_hbm.at[at], got_ref.at[sy, sx], got_sem.at[sy, sx])

    def side_copy(i, half):
        return pltpu.make_async_copy(
            side_hbm[i].at[half], sides[i].at[half], side_sem.at[i, half]
        )

    order = [(sx, sy) for sx in range(nx) for sy in range(nyh)]
    for sx, sy in order:
        got_copy(sy, sx).start()
    total[...] = jnp.zeros_like(total)

    for k, (sx, sy) in enumerate(order):
        got_copy(sy, sx).wait()
        if k == 0:
            for i in range(12):
                side_copy(i, 0).start()
        for d in range(nd):
            yl, co, j = d // (nco * dl), d // dl % nco, d % dl
            parts = [got_ref[sy, sx, at_z ^ sz, yl, co, j] for sz in range(nz)]
            turned[d * nb : (d + 1) * nb, k * run : (k + 1) * run] = jnp.transpose(
                jnp.concatenate(parts, axis=0)
            )

    @pl.loop(0, nyl)
    def _(half):
        for i in range(10):
            side_copy(i, half).wait()

        @pl.when(half + 1 < nyl)
        def _():
            for i in range(12):
                side_copy(i, half + 1).start()

        @pl.loop(0, AROWS)
        def _(arow):
            weights = jnp.concatenate(
                [
                    jnp.concatenate(
                        [piece[half, :, :, arow].reshape(-1, nc) for piece in pieces], axis=0
                    )
                    for pieces in (sides[:5], sides[5:10])
                ],
                axis=1,
            )
            panel = jnp.dot(turned[...], weights, preferred_element_type=jnp.float32)
            panel = panel.astype(jnp.bfloat16)
            row = pl.multiple_of(arow * nb, nb)
            for co in range(nco):
                for d in range(nd):
                    panels[pl.ds(row, nb), (co * nd + d) * nc : (co * nd + d + 1) * nc] = panel[
                        d * nb : (d + 1) * nb, co * nc : (co + 1) * nc
                    ]

        for i in range(10, 12):
            side_copy(i, half).wait()
        for co in range(nco):
            total[...] += jnp.dot(
                panels[:, co * nd * nc : (co + 1) * nd * nc],
                sides[10 + co][half].reshape(nd * nc, npair),
                preferred_element_type=jnp.float32,
            )

    out_ref[...] = jnp.transpose(total[...].astype(jnp.bfloat16))


def make_ladder(where, got, pairs, amps):
    nyh, nx, nz, nyl, nco, _, nl, nb = got.shape
    nd, nc, npair = amps[0].shape[1:]
    deep = nyh * nx * nz * nl
    sides = list(pairs) + list(amps)
    return pl.pallas_call(
        ladder_kernel,
        in_specs=[pl.BlockSpec(memory_space=pltpu.SMEM)]
        + [pl.BlockSpec(memory_space=pl.ANY)] * 13,
        out_specs=pl.BlockSpec(memory_space=pltpu.VMEM),
        scratch_shapes=[pltpu.VMEM(side.shape, side.dtype) for side in [got] + sides]
        + [
            pltpu.VMEM((nd * nb, deep), jnp.bfloat16),
            pltpu.VMEM((AROWS * nb, nco * nd * nc), jnp.bfloat16),
            pltpu.VMEM((AROWS * nb, npair), jnp.float32),
            pltpu.SemaphoreType.DMA((nyh, nx)),
            pltpu.SemaphoreType.DMA((12, nyl)),
        ],
        out_shape=jax.ShapeDtypeStruct((npair, AROWS * nb), jnp.bfloat16),
        name="ladder",
    )(where, got, *sides)


def body(half, mo, amp):
    nl, _, nc = half.shape
    nv = mo.shape[1]
    npair = amp.shape[3]
    lanes = SIZES["yh"] * SIZES["x"] * SIZES["z"]
    groups = SIZES["yl"] * SIZES["co"]
    dl, nb = nc // lanes, nv // groups

    pair = jnp.einsum("lmc,ma->alc", half, mo[:, :AROWS], preferred_element_type=jnp.float32)
    pair = pair.astype(jnp.bfloat16)[None]
    half, pair, amp = lax.optimization_barrier((half, pair, amp))
    amp = jnp.transpose(amp.reshape(nc, groups * dl, npair), (1, 0, 2))[None]
    amp_far = swap(amp, "yl", 1)
    send = make_vec(half, mo, lanes, groups, 0)
    pair = double(pair, "z", 1)
    send, pair = lax.optimization_barrier((send, pair))
    send = make_vec(half, mo, lanes, groups, 1, send)
    pair = double(pair, "z", 2)
    pair = double(pair, "z", 4)
    send, pair = lax.optimization_barrier((send, pair))
    send = send.reshape(lanes * groups, dl * nl, nb)
    got = lax.all_to_all(send, EVERY, 0, 0, tiled=True)
    got = got.reshape(2, 4, 8, 2, 2, dl, nl, nb)
    pair = pair[None]
    far = swap(pair, ("yh", "yl"), 2)
    near = swap(pair, ("yh", "yl"), 1)
    cross = swap(pair, ("yh", "yl"), 3)
    pair = jnp.concatenate([pair, far, near, cross], axis=0)
    pair = pair.reshape((2, 2) + pair.shape[1:])
    amp = jnp.concatenate([amp, amp_far], axis=0)
    amps = [amp, swap(amp, "co", 1)]
    one = swap(pair, "x", 1)
    three = swap(pair, "x", 3)
    two = [swap(three[:, :1], "x", 1), swap(one[:, 1:], "x", 3)]
    pieces = [pair, one, two[0], two[1], three]
    pairs = pieces + [swap(piece, "co", 1) for piece in pieces]

    where = jnp.stack([lax.axis_index("yh"), lax.axis_index("x"), lax.axis_index("z")])
    part = make_ladder(where.astype(jnp.int32), got, pairs, amps)
    part = lax.all_to_all(
        part.reshape(lanes, npair // lanes, AROWS * nb), LANE, 0, 0, tiled=True
    )
    part = jnp.sum(part.astype(jnp.float32), axis=0)
    return part.reshape(npair // lanes, AROWS, nb)


def solution(mesh):
    fine = Mesh(mesh.devices.reshape(tuple(SIZES.values())), EVERY)
    in_specs = (P(LANE, None, GROUP), P(), P(GROUP, None, LANE, None))
    out_specs = P(LANE, None, GROUP)
    return jax.shard_map(
        body, mesh=fine, in_specs=in_specs, out_specs=out_specs, check_vma=False
    )
```

```python
import jax
import jax.numpy as jnp
from jax import lax
from jax.experimental import pallas as pl
from jax.experimental.pallas import tpu as pltpu
from jax.sharding import Mesh, PartitionSpec as P


AROWS = 4
LANE = ("yh", "x", "z")
GROUP = ("yl", "co")
EVERY = LANE + GROUP
PHASES = 2
Z_STEPS = (1, 2, 7)
Z_OFF = (0, 1, 2, 3, 7, 6, 5, 4)
SIZES = {"yh": 2, "x": 4, "z": 8, "yl": 2, "co": 2}


def swap(block, axis, flip):
    count = 4 if isinstance(axis, tuple) else SIZES[axis]
    return lax.ppermute(block, axis, [(i, i ^ flip) for i in range(count)])


def double(block, axis, flip):
    return jnp.concatenate([block, swap(block, axis, flip)], axis=0)


def vec_kernel(half_ref, mo_ref, *refs):
    send_ref, rows = refs[-2:]
    part, _, nc = half_ref.shape
    lanes, groups, dl, step, nb = send_ref.shape
    now = pl.program_id(0)

    @pl.when(now < PHASES)
    def _():
        for i in range(part):
            full = lax.dot_general(
                half_ref[i], mo_ref[...], (((0,), (0,)), ((), ())),
                preferred_element_type=jnp.float32,
            )
            row = pl.multiple_of((now * part + i) * nc, nc)
            for g in range(groups):
                rows[g, pl.ds(row, nc), :] = full[:, g * nb : (g + 1) * nb]

    @pl.when(now >= PHASES)
    def _():
        first = (now - PHASES) * lanes * dl

        @pl.loop(0, lanes, unroll=8)
        def _(lane):
            for j in range(dl):
                for g in range(groups):
                    piece = rows[g, pl.ds(first + lane * dl + j, step, stride=nc), :]
                    send_ref[lane, g, j] = piece.astype(send_ref.dtype)


def make_vec(half, mo, lanes, groups, which, send=None):
    nl, nao, nc = half.shape
    nv = mo.shape[1]
    dl, nb = nc // lanes, nv // groups
    step = nl // 2
    ins = [
        pl.BlockSpec(
            (step // PHASES, nao, nc),
            lambda i: (which * PHASES + jnp.minimum(i, PHASES - 1), 0, 0),
        ),
        pl.BlockSpec((nao, nv), lambda i: (0, 0)),
    ]
    args = (half, mo)
    if send is not None:
        ins.append(pl.BlockSpec(memory_space=pl.ANY))
        args += (send,)
    return pl.pallas_call(
        vec_kernel,
        grid=(2 * PHASES,),
        in_specs=ins,
        out_specs=pl.BlockSpec(
            (lanes // PHASES, groups, dl, step, nb),
            lambda i: (jnp.maximum(i - PHASES, 0), 0, 0, which, 0),
        ),
        out_shape=jax.ShapeDtypeStruct((lanes, groups, dl, nl, nb), jnp.bfloat16),
        scratch_shapes=[pltpu.VMEM((groups, step * nc, nb), jnp.float32)],
        input_output_aliases={2: 0} if send is not None else {},
        cost_estimate=pl.CostEstimate(
            flops=2 * step * nao * nc * nv,
            transcendentals=0,
            bytes_accessed=2 * step * (nao * nc + nc * nv),
        ),
        name="vec",
    )(*args)


def ladder_kernel(where_ref, got_hbm, *refs):
    turned, panels, total, got_sem, side_sem = refs[-5:]
    count = side_sem.shape[0]
    side_hbm, out_ref, got_ref, sides = refs[:count], refs[count], refs[count + 1], refs[count + 2 : -5]
    nyh, nx, nz, nyl, nco, dl, nl, nb = got_ref.shape
    nd = nyl * nco * dl
    nc, npair = sides[-1].shape[-2:]
    run = nz * nl
    at_yh, at_x, at_z = where_ref[0], where_ref[1], where_ref[2]

    def got_copy(sy, sx):
        at = (at_yh ^ sy, at_x ^ sx)
        return pltpu.make_async_copy(got_hbm.at[at], got_ref.at[sy, sx], got_sem.at[sy, sx])

    def side_copy(i, half):
        source = 1 - half if i < count - nco and i % nyh else half
        return pltpu.make_async_copy(
            side_hbm[i].at[source], sides[i].at[half], side_sem.at[i, half]
        )

    order = [(sx, sy) for sx in range(nx) for sy in range(nyh)]
    for sx, sy in order:
        got_copy(sy, sx).start()
    total[...] = jnp.zeros_like(total)

    for k, (sx, sy) in enumerate(order):
        got_copy(sy, sx).wait()
        if k == 0:
            for i in range(count):
                side_copy(i, 0).start()
        for d in range(nd):
            yl, co, j = d // (nco * dl), d // dl % nco, d % dl
            parts = [got_ref[sy, sx, at_z ^ Z_OFF[sz], yl, co, j] for sz in range(nz)]
            turned[d * nb : (d + 1) * nb, k * run : (k + 1) * run] = jnp.transpose(
                jnp.concatenate(parts, axis=0)
            )

    @pl.loop(0, nyl)
    def _(half):
        for i in range(count - nco):
            side_copy(i, half).wait()

        @pl.when(half + 1 < nyl)
        def _():
            for i in range(count):
                side_copy(i, half + 1).start()

        @pl.loop(0, AROWS)
        def _(arow):
            weights = jnp.concatenate(
                [
                    jnp.concatenate(
                        [piece[half, :, arow].reshape(-1, nc) for piece in pieces], axis=0
                    )
                    for pieces in (sides[: count // 2 - 1], sides[count // 2 - 1 : -2])
                ],
                axis=1,
            )
            panel = jnp.dot(turned[...], weights, preferred_element_type=jnp.float32)
            panel = panel.astype(jnp.bfloat16)
            row = pl.multiple_of(arow * nb, nb)
            for co in range(nco):
                for d in range(nd):
                    panels[pl.ds(row, nb), (co * nd + d) * nc : (co * nd + d + 1) * nc] = panel[
                        d * nb : (d + 1) * nb, co * nc : (co + 1) * nc
                    ]

        for i in range(count - nco, count):
            side_copy(i, half).wait()
        for co in range(nco):
            total[...] += jnp.dot(
                panels[:, co * nd * nc : (co + 1) * nd * nc],
                sides[count - nco + co][half].reshape(nd * nc, npair),
                preferred_element_type=jnp.float32,
            )

    out_ref[...] = jnp.transpose(total[...].astype(jnp.bfloat16))


def make_ladder(where, got, pairs, amps):
    nyh, nx, nz, nyl, nco, _, nl, nb = got.shape
    nd, nc, npair = amps[0].shape[1:]
    deep = nyh * nx * nz * nl
    sides = list(pairs) + list(amps)
    return pl.pallas_call(
        ladder_kernel,
        in_specs=[pl.BlockSpec(memory_space=pltpu.SMEM)]
        + [pl.BlockSpec(memory_space=pl.ANY)] * (1 + len(sides)),
        out_specs=pl.BlockSpec(memory_space=pltpu.VMEM),
        scratch_shapes=[pltpu.VMEM(side.shape, side.dtype) for side in [got] + sides]
        + [
            pltpu.VMEM((nd * nb, deep), jnp.bfloat16),
            pltpu.VMEM((AROWS * nb, nco * nd * nc), jnp.bfloat16),
            pltpu.VMEM((AROWS * nb, npair), jnp.float32),
            pltpu.SemaphoreType.DMA((nyh, nx)),
            pltpu.SemaphoreType.DMA((len(sides), nyl)),
        ],
        out_shape=jax.ShapeDtypeStruct((npair, AROWS * nb), jnp.bfloat16),
        compiler_params=pltpu.CompilerParams(vmem_limit_bytes=34 << 20),
        name="ladder",
    )(where, got, *sides)


def body(half, mo, amp):
    nl, _, nc = half.shape
    nv = mo.shape[1]
    npair = amp.shape[3]
    lanes = SIZES["yh"] * SIZES["x"] * SIZES["z"]
    groups = SIZES["yl"] * SIZES["co"]
    dl, nb = nc // lanes, nv // groups

    pair = jnp.einsum("lmc,ma->alc", half, mo[:, :AROWS], preferred_element_type=jnp.float32)
    pair = pair.astype(jnp.bfloat16)[None]
    half, pair, amp = lax.optimization_barrier((half, pair, amp))
    amp = jnp.transpose(amp.reshape(nc, groups * dl, npair), (1, 0, 2))[None]
    amp_far = swap(amp, "yl", 1)
    send = make_vec(half, mo, lanes, groups, 0)
    pair = double(pair, "z", Z_STEPS[0])
    send, pair = lax.optimization_barrier((send, pair))
    send = make_vec(half, mo, lanes, groups, 1, send)
    pair = double(pair, "z", Z_STEPS[1])
    pair = double(pair, "z", Z_STEPS[2])
    send, pair = lax.optimization_barrier((send, pair))
    send = send.reshape(lanes * groups, dl * nl, nb)
    got = lax.all_to_all(send, EVERY, 0, 0, tiled=True)
    got = got.reshape(2, 4, 8, 2, 2, dl, nl, nb)
    pair = pair[None]
    near = swap(pair, ("yh", "yl"), 1)
    same = [jnp.concatenate([pair, near], axis=0), None]
    same[1] = swap(same[0], ("yh", "yl"), 3)
    one = [swap(same[0], "x", 1), None]
    three = [swap(same[0], "x", 3), None]
    one[1] = swap(same[1], "x", 1)
    three[1] = swap(same[1], "x", 3)
    two = [swap(three[0], "x", 1), swap(one[1], "x", 3)]
    pieces = same + one + two + three
    pairs = pieces + [swap(piece, "co", 1) for piece in pieces]
    amp = jnp.concatenate([amp, amp_far], axis=0)
    amps = [amp, swap(amp, "co", 1)]

    where = jnp.stack([lax.axis_index("yh"), lax.axis_index("x"), lax.axis_index("z")])
    part = make_ladder(where.astype(jnp.int32), got, pairs, amps)
    part = lax.all_to_all(
        part.reshape(lanes, npair // lanes, AROWS * nb), LANE, 0, 0, tiled=True
    )
    part = jnp.sum(part.astype(jnp.float32), axis=0)
    return part.reshape(npair // lanes, AROWS, nb)


def solution(mesh):
    fine = Mesh(mesh.devices.reshape(tuple(SIZES.values())), EVERY)
    in_specs = (P(LANE, None, GROUP), P(), P(GROUP, None, LANE, None))
    out_specs = P(LANE, None, GROUP)
    return jax.shard_map(
        body, mesh=fine, in_specs=in_specs, out_specs=out_specs, check_vma=False
    )
```

```python
import jax
import jax.numpy as jnp
from jax import lax
from jax.experimental import pallas as pl
from jax.experimental.pallas import tpu as pltpu
from jax.sharding import Mesh, PartitionSpec as P


AROWS = 4
LANE = ("yh", "x", "z")
GROUP = ("yl", "co")
EVERY = LANE + GROUP
PHASES = 2
Z_STEPS = (1, 2, 7)
Z_OFF = (0, 1, 2, 3, 7, 6, 5, 4)
SIZES = {"yh": 2, "x": 4, "z": 8, "yl": 2, "co": 2}


def swap(block, axis, flip):
    count = 4 if isinstance(axis, tuple) else SIZES[axis]
    return lax.ppermute(block, axis, [(i, i ^ flip) for i in range(count)])


def double(block, axis, flip):
    return jnp.concatenate([block, swap(block, axis, flip)], axis=0)


def vec_kernel(half_ref, mo_ref, *refs):
    send_ref, rows = refs[-2:]
    part, _, nc = half_ref.shape
    lanes, groups, dl, step, nb = send_ref.shape
    now = pl.program_id(0)

    @pl.when(now < PHASES)
    def _():
        for i in range(part):
            full = lax.dot_general(
                half_ref[i], mo_ref[...], (((0,), (0,)), ((), ())),
                preferred_element_type=jnp.float32,
            )
            row = pl.multiple_of((now * part + i) * nc, nc)
            for g in range(groups):
                rows[g, pl.ds(row, nc), :] = full[:, g * nb : (g + 1) * nb]

    @pl.when(now >= PHASES)
    def _():
        first = (now - PHASES) * lanes * dl

        @pl.loop(0, lanes, unroll=8)
        def _(lane):
            for j in range(dl):
                for g in range(groups):
                    piece = rows[g, pl.ds(first + lane * dl + j, step, stride=nc), :]
                    send_ref[lane, g, j] = piece.astype(send_ref.dtype)


def make_vec(half, mo, lanes, groups, which, send=None):
    nl, nao, nc = half.shape
    nv = mo.shape[1]
    dl, nb = nc // lanes, nv // groups
    step = nl // 2
    ins = [
        pl.BlockSpec(
            (step // PHASES, nao, nc),
            lambda i: (which * PHASES + jnp.minimum(i, PHASES - 1), 0, 0),
        ),
        pl.BlockSpec((nao, nv), lambda i: (0, 0)),
    ]
    args = (half, mo)
    if send is not None:
        ins.append(pl.BlockSpec(memory_space=pl.ANY))
        args += (send,)
    return pl.pallas_call(
        vec_kernel,
        grid=(2 * PHASES,),
        in_specs=ins,
        out_specs=pl.BlockSpec(
            (lanes // PHASES, groups, dl, step, nb),
            lambda i: (jnp.maximum(i - PHASES, 0), 0, 0, which, 0),
        ),
        out_shape=jax.ShapeDtypeStruct((lanes, groups, dl, nl, nb), jnp.bfloat16),
        scratch_shapes=[pltpu.VMEM((groups, step * nc, nb), jnp.float32)],
        input_output_aliases={2: 0} if send is not None else {},
        cost_estimate=pl.CostEstimate(
            flops=2 * step * nao * nc * nv,
            transcendentals=0,
            bytes_accessed=2 * step * (nao * nc + nc * nv),
        ),
        name="vec",
    )(*args)


def ladder_kernel(where_ref, got_hbm, *refs):
    turned, panels, total, got_sem, side_sem = refs[-5:]
    count = side_sem.shape[0]
    side_hbm, out_ref, got_ref, sides = refs[:count], refs[count], refs[count + 1], refs[count + 2 : -5]
    nyh, nx, nz, nyl, nco, dl, nl, nb = got_ref.shape
    nd = nyl * nco * dl
    nc, npair = sides[-1].shape[-2:]
    run = nz * nl
    at_yh, at_x, at_z = where_ref[0], where_ref[1], where_ref[2]

    def got_copy(sy, sx):
        at = (at_yh ^ sy, at_x ^ sx)
        return pltpu.make_async_copy(got_hbm.at[at], got_ref.at[sy, sx], got_sem.at[sy, sx])

    def side_copy(i, half):
        return pltpu.make_async_copy(
            side_hbm[i].at[half], sides[i].at[half], side_sem.at[i, half]
        )

    order = [(sx, sy) for sx in range(nx) for sy in range(nyh)]
    for sx, sy in order:
        got_copy(sy, sx).start()
    total[...] = jnp.zeros_like(total)

    for k, (sx, sy) in enumerate(order):
        got_copy(sy, sx).wait()
        if k == 0:
            for i in range(count):
                side_copy(i, 0).start()
        for d in range(nd):
            yl, co, j = d // (nco * dl), d // dl % nco, d % dl
            parts = [got_ref[sy, sx, at_z ^ Z_OFF[sz], yl, co, j] for sz in range(nz)]
            turned[d * nb : (d + 1) * nb, k * run : (k + 1) * run] = jnp.transpose(
                jnp.concatenate(parts, axis=0)
            )

    @pl.loop(0, nyl)
    def _(half):
        for i in range(count - nco):
            side_copy(i, half).wait()

        @pl.when(half + 1 < nyl)
        def _():
            for i in range(count):
                side_copy(i, half + 1).start()

        @pl.loop(0, AROWS)
        def _(arow):
            weights = jnp.concatenate(
                [
                    jnp.concatenate(
                        [piece[half, :, arow].reshape(-1, nc) for piece in pieces], axis=0
                    )
                    for pieces in (sides[: count // 2 - 1], sides[count // 2 - 1 : -2])
                ],
                axis=1,
            )
            panel = jnp.dot(turned[...], weights, preferred_element_type=jnp.float32)
            panel = panel.astype(jnp.bfloat16)
            row = pl.multiple_of(arow * nb, nb)
            for co in range(nco):
                for d in range(nd):
                    panels[pl.ds(row, nb), (co * nd + d) * nc : (co * nd + d + 1) * nc] = panel[
                        d * nb : (d + 1) * nb, co * nc : (co + 1) * nc
                    ]

        for i in range(count - nco, count):
            side_copy(i, half).wait()
        for co in range(nco):
            total[...] += jnp.dot(
                panels[:, co * nd * nc : (co + 1) * nd * nc],
                sides[count - nco + co][half].reshape(nd * nc, npair),
                preferred_element_type=jnp.float32,
            )

    out_ref[...] = jnp.transpose(total[...].astype(jnp.bfloat16))


def make_ladder(where, got, pairs, amps):
    nyh, nx, nz, nyl, nco, _, nl, nb = got.shape
    nd, nc, npair = amps[0].shape[1:]
    deep = nyh * nx * nz * nl
    sides = list(pairs) + list(amps)
    return pl.pallas_call(
        ladder_kernel,
        in_specs=[pl.BlockSpec(memory_space=pltpu.SMEM)]
        + [pl.BlockSpec(memory_space=pl.ANY)] * (1 + len(sides)),
        out_specs=pl.BlockSpec(memory_space=pltpu.VMEM),
        scratch_shapes=[pltpu.VMEM(side.shape, side.dtype) for side in [got] + sides]
        + [
            pltpu.VMEM((nd * nb, deep), jnp.bfloat16),
            pltpu.VMEM((AROWS * nb, nco * nd * nc), jnp.bfloat16),
            pltpu.VMEM((AROWS * nb, npair), jnp.float32),
            pltpu.SemaphoreType.DMA((nyh, nx)),
            pltpu.SemaphoreType.DMA((len(sides), nyl)),
        ],
        out_shape=jax.ShapeDtypeStruct((npair, AROWS * nb), jnp.bfloat16),
        compiler_params=pltpu.CompilerParams(vmem_limit_bytes=34 << 20),
        name="ladder",
    )(where, got, *sides)


def body(half, mo, amp):
    nl, _, nc = half.shape
    nv = mo.shape[1]
    npair = amp.shape[3]
    lanes = SIZES["yh"] * SIZES["x"] * SIZES["z"]
    groups = SIZES["yl"] * SIZES["co"]
    dl, nb = nc // lanes, nv // groups

    pair = jnp.einsum("lmc,ma->alc", half, mo[:, :AROWS], preferred_element_type=jnp.float32)
    pair = pair.astype(jnp.bfloat16)[None]
    half, pair, amp = lax.optimization_barrier((half, pair, amp))
    amp = jnp.transpose(amp.reshape(nc, groups * dl, npair), (1, 0, 2))[None]
    amp_far = swap(amp, "yl", 1)
    send = make_vec(half, mo, lanes, groups, 0)
    pair = double(pair, "z", Z_STEPS[0])
    send, pair = lax.optimization_barrier((send, pair))
    send = make_vec(half, mo, lanes, groups, 1, send)
    pair = double(pair, "z", Z_STEPS[1])
    pair = double(pair, "z", Z_STEPS[2])
    send, pair = lax.optimization_barrier((send, pair))
    send = send.reshape(lanes * groups, dl * nl, nb)
    got = lax.all_to_all(send, EVERY, 0, 0, tiled=True)
    got = got.reshape(2, 4, 8, 2, 2, dl, nl, nb)
    pair = pair[None]
    near = swap(pair, ("yh", "yl"), 1)
    far = swap(pair, ("yh", "yl"), 2)
    cross = swap(pair, ("yh", "yl"), 3)
    same = [jnp.concatenate([pair, near], axis=0), jnp.concatenate([far, cross], axis=0)]
    one = [swap(same[0], "x", 1), None]
    three = [swap(same[0], "x", 3), None]
    one[1] = swap(same[1], "x", 1)
    three[1] = swap(same[1], "x", 3)
    two = [swap(three[0], "x", 1), swap(one[1], "x", 3)]
    pieces = same + one + two + three
    pairs = pieces + [swap(piece, "co", 1) for piece in pieces]
    amp = jnp.concatenate([amp, amp_far], axis=0)
    amps = [amp, swap(amp, "co", 1)]

    where = jnp.stack([lax.axis_index("yh"), lax.axis_index("x"), lax.axis_index("z")])
    part = make_ladder(where.astype(jnp.int32), got, pairs, amps)
    part = lax.all_to_all(
        part.reshape(lanes, npair // lanes, AROWS * nb), LANE, 0, 0, tiled=True
    )
    part = jnp.sum(part.astype(jnp.float32), axis=0)
    return part.reshape(npair // lanes, AROWS, nb)


def solution(mesh):
    fine = Mesh(mesh.devices.reshape(tuple(SIZES.values())), EVERY)
    in_specs = (P(LANE, None, GROUP), P(), P(GROUP, None, LANE, None))
    out_specs = P(LANE, None, GROUP)
    return jax.shard_map(
        body, mesh=fine, in_specs=in_specs, out_specs=out_specs, check_vma=False
    )
```

```python
import jax
import jax.numpy as jnp
from jax import lax
from jax.experimental import pallas as pl
from jax.experimental.pallas import tpu as pltpu
from jax.sharding import Mesh, PartitionSpec as P


AROWS = 4
LANE = ("yh", "x", "z")
GROUP = ("yl", "co")
EVERY = LANE + GROUP
PHASES = 2
Z_STEPS = (1, 2, 6)
Z_OFF = (0, 1, 2, 3, 6, 7, 4, 5)
SIZES = {"yh": 2, "x": 4, "z": 8, "yl": 2, "co": 2}


def swap(block, axis, flip):
    count = 4 if isinstance(axis, tuple) else SIZES[axis]
    return lax.ppermute(block, axis, [(i, i ^ flip) for i in range(count)])


def double(block, axis, flip):
    return jnp.concatenate([block, swap(block, axis, flip)], axis=0)


def vec_kernel(half_ref, mo_ref, *refs):
    send_ref, rows = refs[-2:]
    part, _, nc = half_ref.shape
    lanes, groups, dl, step, nb = send_ref.shape
    now = pl.program_id(0)

    @pl.when(now < PHASES)
    def _():
        for i in range(part):
            full = lax.dot_general(
                half_ref[i], mo_ref[...], (((0,), (0,)), ((), ())),
                preferred_element_type=jnp.float32,
            )
            row = pl.multiple_of((now * part + i) * nc, nc)
            for g in range(groups):
                rows[g, pl.ds(row, nc), :] = full[:, g * nb : (g + 1) * nb]

    @pl.when(now >= PHASES)
    def _():
        first = (now - PHASES) * lanes * dl

        @pl.loop(0, lanes, unroll=16)
        def _(lane):
            for j in range(dl):
                for g in range(groups):
                    piece = rows[g, pl.ds(first + lane * dl + j, step, stride=nc), :]
                    send_ref[lane, g, j] = piece.astype(send_ref.dtype)


def make_vec(half, mo, lanes, groups, which, send=None):
    nl, nao, nc = half.shape
    nv = mo.shape[1]
    dl, nb = nc // lanes, nv // groups
    step = nl // 2
    ins = [
        pl.BlockSpec(
            (step // PHASES, nao, nc),
            lambda i: (which * PHASES + jnp.minimum(i, PHASES - 1), 0, 0),
        ),
        pl.BlockSpec((nao, nv), lambda i: (0, 0)),
    ]
    args = (half, mo)
    if send is not None:
        ins.append(pl.BlockSpec(memory_space=pl.ANY))
        args += (send,)
    return pl.pallas_call(
        vec_kernel,
        grid=(2 * PHASES,),
        in_specs=ins,
        out_specs=pl.BlockSpec(
            (lanes // PHASES, groups, dl, step, nb),
            lambda i: (jnp.maximum(i - PHASES, 0), 0, 0, which, 0),
        ),
        out_shape=jax.ShapeDtypeStruct((lanes, groups, dl, nl, nb), jnp.bfloat16),
        scratch_shapes=[pltpu.VMEM((groups, step * nc, nb), jnp.float32)],
        input_output_aliases={2: 0} if send is not None else {},
        cost_estimate=pl.CostEstimate(
            flops=2 * step * nao * nc * nv,
            transcendentals=0,
            bytes_accessed=2 * step * (nao * nc + nc * nv),
        ),
        name="vec",
    )(*args)


def ladder_kernel(where_ref, got_hbm, *refs):
    turned, panels, total, got_sem, side_sem = refs[-5:]
    count = side_sem.shape[0]
    side_hbm, out_ref, got_ref, sides = refs[:count], refs[count], refs[count + 1], refs[count + 2 : -5]
    nyh, nx, nz, nyl, nco, dl, nl, nb = got_ref.shape
    nd = nyl * nco * dl
    nc, npair = sides[-1].shape[-2:]
    run = nz * nl
    at_yh, at_x, at_z = where_ref[0], where_ref[1], where_ref[2]

    def got_copy(sy, sx):
        at = (at_yh ^ sy, at_x ^ sx)
        return pltpu.make_async_copy(got_hbm.at[at], got_ref.at[sy, sx], got_sem.at[sy, sx])

    def side_copy(i, half):
        return pltpu.make_async_copy(
            side_hbm[i].at[half], sides[i].at[half], side_sem.at[i, half]
        )

    order = [(sx, sy) for sx in range(nx) for sy in range(nyh)]
    for sx, sy in order:
        got_copy(sy, sx).start()
    total[...] = jnp.zeros_like(total)

    for k, (sx, sy) in enumerate(order):
        got_copy(sy, sx).wait()
        if k == 0:
            for i in range(count):
                side_copy(i, 0).start()
        for d in range(nd):
            yl, co, j = d // (nco * dl), d // dl % nco, d % dl
            parts = [got_ref[sy, sx, at_z ^ Z_OFF[sz], yl, co, j] for sz in range(nz)]
            turned[d * nb : (d + 1) * nb, k * run : (k + 1) * run] = jnp.transpose(
                jnp.concatenate(parts, axis=0)
            )

    @pl.loop(0, nyl)
    def _(half):
        for i in range(count - nco):
            side_copy(i, half).wait()

        @pl.when(half + 1 < nyl)
        def _():
            for i in range(count):
                side_copy(i, half + 1).start()

        @pl.loop(0, AROWS)
        def _(arow):
            weights = jnp.concatenate(
                [
                    jnp.concatenate(
                        [piece[half, :, arow].reshape(-1, nc) for piece in pieces], axis=0
                    )
                    for pieces in (sides[: count // 2 - 1], sides[count // 2 - 1 : -2])
                ],
                axis=1,
            )
            panel = jnp.dot(turned[...], weights, preferred_element_type=jnp.float32)
            panel = panel.astype(jnp.bfloat16)
            row = pl.multiple_of(arow * nb, nb)
            for co in range(nco):
                for d in range(nd):
                    panels[pl.ds(row, nb), (co * nd + d) * nc : (co * nd + d + 1) * nc] = panel[
                        d * nb : (d + 1) * nb, co * nc : (co + 1) * nc
                    ]

        for i in range(count - nco, count):
            side_copy(i, half).wait()
        for co in range(nco):
            total[...] += jnp.dot(
                panels[:, co * nd * nc : (co + 1) * nd * nc],
                sides[count - nco + co][half].reshape(nd * nc, npair),
                preferred_element_type=jnp.float32,
            )

    out_ref[...] = jnp.transpose(total[...].astype(jnp.bfloat16))


def make_ladder(where, got, pairs, amps):
    nyh, nx, nz, nyl, nco, _, nl, nb = got.shape
    nd, nc, npair = amps[0].shape[1:]
    deep = nyh * nx * nz * nl
    sides = list(pairs) + list(amps)
    return pl.pallas_call(
        ladder_kernel,
        in_specs=[pl.BlockSpec(memory_space=pltpu.SMEM)]
        + [pl.BlockSpec(memory_space=pl.ANY)] * (1 + len(sides)),
        out_specs=pl.BlockSpec(memory_space=pltpu.VMEM),
        scratch_shapes=[pltpu.VMEM(side.shape, side.dtype) for side in [got] + sides]
        + [
            pltpu.VMEM((nd * nb, deep), jnp.bfloat16),
            pltpu.VMEM((AROWS * nb, nco * nd * nc), jnp.bfloat16),
            pltpu.VMEM((AROWS * nb, npair), jnp.float32),
            pltpu.SemaphoreType.DMA((nyh, nx)),
            pltpu.SemaphoreType.DMA((len(sides), nyl)),
        ],
        out_shape=jax.ShapeDtypeStruct((npair, AROWS * nb), jnp.bfloat16),
        compiler_params=pltpu.CompilerParams(vmem_limit_bytes=34 << 20),
        name="ladder",
    )(where, got, *sides)


def body(half, mo, amp):
    nl, _, nc = half.shape
    nv = mo.shape[1]
    npair = amp.shape[3]
    lanes = SIZES["yh"] * SIZES["x"] * SIZES["z"]
    groups = SIZES["yl"] * SIZES["co"]
    dl, nb = nc // lanes, nv // groups

    pair = jnp.einsum("lmc,ma->alc", half, mo[:, :AROWS], preferred_element_type=jnp.float32)
    pair = pair.astype(jnp.bfloat16)[None]
    half, pair, amp = lax.optimization_barrier((half, pair, amp))
    amp = jnp.transpose(amp.reshape(nc, groups * dl, npair), (1, 0, 2))[None]
    amp_far = swap(amp, "yl", 1)
    send = make_vec(half, mo, lanes, groups, 0)
    pair = double(pair, "z", Z_STEPS[0])
    send, pair = lax.optimization_barrier((send, pair))
    send = make_vec(half, mo, lanes, groups, 1, send)
    pair = double(pair, "z", Z_STEPS[1])
    pair = double(pair, "z", Z_STEPS[2])
    send, pair = lax.optimization_barrier((send, pair))
    send = send.reshape(lanes * groups, dl * nl, nb)
    got = lax.all_to_all(send, EVERY, 0, 0, tiled=True)
    got = got.reshape(2, 4, 8, 2, 2, dl, nl, nb)
    pair = pair[None]
    near = swap(pair, ("yh", "yl"), 1)
    far = swap(pair, ("yh", "yl"), 2)
    cross = swap(pair, ("yh", "yl"), 3)
    same = [jnp.concatenate([pair, near], axis=0), jnp.concatenate([far, cross], axis=0)]
    one = [swap(same[0], "x", 1), None]
    three = [swap(same[0], "x", 3), None]
    one[1] = swap(same[1], "x", 1)
    three[1] = swap(same[1], "x", 3)
    two = [swap(three[0], "x", 1), swap(one[1], "x", 3)]
    pieces = same + one + two + three
    pairs = pieces + [swap(piece, "co", 1) for piece in pieces]
    amp = jnp.concatenate([amp, amp_far], axis=0)
    amps = [amp, swap(amp, "co", 1)]

    where = jnp.stack([lax.axis_index("yh"), lax.axis_index("x"), lax.axis_index("z")])
    part = make_ladder(where.astype(jnp.int32), got, pairs, amps)
    part = lax.all_to_all(
        part.reshape(lanes, npair // lanes, AROWS * nb), LANE, 0, 0, tiled=True
    )
    part = jnp.sum(part.astype(jnp.float32), axis=0)
    return part.reshape(npair // lanes, AROWS, nb)


def solution(mesh):
    fine = Mesh(mesh.devices.reshape(tuple(SIZES.values())), EVERY)
    in_specs = (P(LANE, None, GROUP), P(), P(GROUP, None, LANE, None))
    out_specs = P(LANE, None, GROUP)
    return jax.shard_map(
        body, mesh=fine, in_specs=in_specs, out_specs=out_specs, check_vma=False
    )
```
